32 devices in a mesh: dp: 4 (over y, core), seq: 8 (over z, x).
Axes of the slice: x: 2, y: 2, z: 4, core: 2. Of those that a mesh axis runs over, the one named last changes fastest.
Arguments:
- queries: bfloat16 [4, 4096, 4096], P('dp', 'seq'), may hold values from -150 to 150
- keys: bfloat16 [4, 4096, 512], P('dp', 'seq'), may hold values from -6 to 6
- values: bfloat16 [4, 4096, 512], P('dp', 'seq'), may hold values from -6 to 6
- grad_out: bfloat16 [4, 4096, 4096], P('dp', 'seq'), may hold values from -6 to 6
- proj_in: bfloat16 [4, 4096, 256], P('dp', 'seq'), may hold values from -6 to 6
- segments: int32 [4, 4096], P('dp'), may hold values from 0 to 63, never falling along the last dimension, each value on 1 to 128 neighbouring positions
Outputs:
- grad_q_proj: float32 [256, 4096], P('dp', 'seq')
- grad_kv_proj: float32 [256, 1024], P('dp', 'seq')
The draws below stay inside these ranges and needn't reach their ends.
Inputs may be any that keep to these rules, and one draw needn't show every extreme that they name: `segments`: document numbers never fall along a sequence; each document has 1 to 128 tokens, and some document has exactly 128.
All inputs are finite; a program needn't handle non-finite values.
Results may differ from the reference program's by a relative error of at most 0.025.
Values may be sent and summed in bfloat16 or wider, within the bound.
No kernel may reach another device: no remote copies, remote signals or barrier semaphores. Data moves between devices by JAX's collectives and lax.ppermute only.
A program may use at most 128 MiB of HBM per device.

```python
import math
import jax
import jax.numpy as jnp
import numpy as np
from jax import lax

H = 32
KV = 4
HD = 128
RANK = 256
DOC = 128
SEQ_LEN = 4096
SEQS = 4


def paired_draw(key):
    base = jax.random.fold_in(key, 7)
    key_q, key_k = jax.random.split(base, 2)
    queries = jnp.clip(jax.random.normal(key_q, (SEQS, SEQ_LEN, H * HD), jnp.float32), -6.0, 6.0)
    keys = jnp.clip(jax.random.normal(key_k, (SEQS, SEQ_LEN, KV * HD), jnp.float32), -6.0, 6.0)
    return (queries, keys)


def draw_queries(key, part):
    return paired_draw(key)[0].astype(jnp.bfloat16)


def draw_keys(key, part):
    return paired_draw(key)[1].astype(jnp.bfloat16)


def strengthened(values, rng, source, target, shards_of, factor):
    def block_of(axis_at):
        return (jnp.arange(values.shape[axis_at]) // (values.shape[axis_at] // shards_of)).reshape((-1,) + (1,) * (values.ndim - 1 - axis_at))

    one_side = jax.random.permutation(rng, shards_of)[block_of(target)]
    other_side = (block_of(target) + shards_of // 2) % shards_of
    return jnp.where((block_of(source) == one_side) | (block_of(source) == other_side), factor * values, values)


def steps_of(stream_key, shape, pieces, low, top_value):
    loudness = 1.0
    for position, blocks in pieces:
        steps = jax.random.uniform(jax.random.fold_in(jax.random.fold_in(stream_key, 6), position), (blocks,), jnp.float32, low / len(pieces), top_value / len(pieces))
        loudness = loudness * jnp.repeat(jnp.exp(steps), shape[position] // blocks).reshape((-1,) + (1,) * (len(shape) - 1 - position))
    return loudness


def split_up(count, total, bound, lean):
    loads = [(1 << 20) // math.isqrt(rank ** lean) + 1 for rank in range(2, count + 1)]
    spare, given = total - bound - (count - 1), [1] * (count - 1)
    while spare > 0:
        movable = [i for i in range(count - 1) if given[i] < bound]
        pool, left = sum([loads[i] for i in movable]), spare
        for i in movable:
            more = min(bound - given[i], max(1, left * loads[i] // pool), spare)
            given[i] = given[i] + more
            spare = spare - more
    return np.array([bound] + given)


def uneven(rng, amount, total, bound, skew):
    if amount == 2:
        one = jax.random.randint(rng, (), max(1, total - bound), min(bound, total - 1) + 1)
        return jnp.stack([one, total - one])
    sizes = jnp.asarray(split_up(amount, total, bound, skew), jnp.int32)
    pairs = (amount - 1) // 2
    source_of, taker = sizes[1:1 + 2 * pairs:2], sizes[2:2 + 2 * pairs:2]
    margin = jnp.minimum(source_of - 1, bound - taker)
    passed = jax.random.randint(jax.random.fold_in(rng, 1), (pairs,), 0, 1 << 20) % (margin + 1)
    sizes = sizes.at[1:1 + 2 * pairs:2].set(source_of - passed).at[2:2 + 2 * pairs:2].set(taker + passed)
    return sizes[jax.random.permutation(jax.random.fold_in(rng, 2), amount)]


def gaussian(own_key, shape, deviation, most, cuts=(), held_as=jnp.bfloat16):
    level = steps_of(own_key, shape, cuts, -0.22, 0.18) if cuts else 1.0
    result = jax.random.normal(own_key, shape, jnp.float32) * deviation * level
    return jnp.minimum(jnp.maximum(result, -most), most).astype(held_as)


def noise_with(key, shape, scale, limit, cuts, heavy, dtype=jnp.bfloat16):
    result = scale * jax.random.normal(key, shape, jnp.float32)
    if cuts:
        result = result * steps_of(key, shape, cuts, -0.22, 0.18)
    return jnp.clip(strengthened(result, jax.random.fold_in(key, 3), *heavy), -limit, limit).astype(dtype)


def setup_inputs(seed: int = 0) -> dict:
    seeds = jax.random.split(jax.random.key(seed), 7)
    queries = draw_queries(jax.random.fold_in(seeds[6], 71), 0)
    keys = draw_keys(jax.random.fold_in(seeds[6], 71), 0)
    values = gaussian(seeds[2], (SEQS, SEQ_LEN, KV * HD), 1.0, 6.0, ((0, 4), (1, 8)))
    grad_out = gaussian(seeds[3], (SEQS, SEQ_LEN, H * HD), 1.0, 6.0, ((0, 4), (1, 8)))
    proj_in = noise_with(seeds[4], (SEQS, SEQ_LEN, RANK), 1.0, 6.0, ((0, 4), (1, 8)), (0, 2, 4, 2.0))
    segments = jax.vmap(lambda own: jnp.searchsorted(jnp.cumsum(uneven(own, 2 * SEQ_LEN // DOC, SEQ_LEN, DOC, 1)), jnp.arange(SEQ_LEN), side="right"))(jax.random.split(seeds[5], SEQS)).reshape((SEQS, SEQ_LEN)).astype(jnp.int32)
    return {"queries": queries, "keys": keys, "values": values, "grad_out": grad_out, "proj_in": proj_in, "segments": segments}


def shifted_window(blocks, filler):
    previous = jnp.concatenate([jnp.full_like(blocks[:1], filler), blocks[:-1]], axis=0)
    return jnp.concatenate([previous, blocks], axis=1)


def attend(q_heads, k_heads, v_heads, g_heads, segment):
    length = q_heads.shape[0]
    head_count = q_heads.shape[1]
    head_width = q_heads.shape[2]
    block_count = length // DOC
    group_size = min(512 // DOC, block_count)
    scaling = head_width ** -0.5

    def to_blocks(array):
        return array.reshape((block_count, DOC) + array.shape[1:])

    def grouped(array):
        return array.reshape((block_count // group_size, group_size) + array.shape[1:])

    seg_query = to_blocks(segment)
    seg_key = shifted_window(seg_query, -1)
    q_block = to_blocks(q_heads)
    g_block = to_blocks(g_heads)
    k_window = shifted_window(to_blocks(k_heads), 0.0)
    v_window = shifted_window(to_blocks(v_heads), 0.0)
    causal = jnp.arange(2 * DOC)[None, :] <= jnp.arange(DOC)[:, None] + DOC

    def one_group(items):
        q_part, g_part, k_part, v_part, sq_part, sk_part = items
        q_part = q_part.astype(jnp.float32)
        g_part = g_part.astype(jnp.float32)
        k_part = k_part.astype(jnp.float32)
        v_part = v_part.astype(jnp.float32)
        allowed = (sq_part[:, :, None] == sk_part[:, None, :]) & causal[None]
        allowed = allowed[:, None]
        scores = jnp.einsum('nqhd,nkhd->nhqk', q_part, k_part) * scaling
        scores = jnp.where(allowed, scores, -1e30)
        probs = jnp.exp(scores - jnp.max(scores, axis=-1, keepdims=True))
        probs = jnp.where(allowed, probs, 0.0)
        probs = probs / jnp.sum(probs, axis=-1, keepdims=True)
        probs_b = probs.astype(jnp.bfloat16)
        attn_out = jnp.einsum('nhqk,nkhd->nqhd', probs_b.astype(jnp.float32), v_part).astype(jnp.bfloat16)
        delta = jnp.sum(g_part * attn_out.astype(jnp.float32), axis=-1)
        dprobs = jnp.einsum('nqhd,nkhd->nhqk', g_part, v_part)
        dscore = (probs * (dprobs - jnp.transpose(delta, (0, 2, 1))[..., None]) * scaling).astype(jnp.bfloat16)
        dq_part = jnp.einsum('nhqk,nkhd->nqhd', dscore.astype(jnp.float32), k_part).astype(jnp.bfloat16)
        dk_part = jnp.einsum('nhqk,nqhd->nkhd', dscore.astype(jnp.float32), q_part)
        dv_part = jnp.einsum('nhqk,nqhd->nkhd', probs_b.astype(jnp.float32), g_part)
        return dq_part, dk_part, dv_part

    items = tuple(grouped(array) for array in (q_block, g_block, k_window, v_window, seg_query, seg_key))
    dq_all, dk_window, dv_window = lax.map(one_group, items)
    dq_all = dq_all.reshape(length, head_count, head_width)

    def fold_window(window):
        window = window.reshape((block_count, 2 * DOC, head_count, head_width))
        later = jnp.concatenate([window[1:, :DOC], jnp.zeros_like(window[:1, :DOC])], axis=0)
        return (window[:, DOC:] + later).reshape(length, head_count, head_width).astype(jnp.bfloat16)

    return dq_all, fold_window(dk_window), fold_window(dv_window)


def reference(queries, keys, values, grad_out, proj_in, segments):
    per_group = H // KV

    def one_sequence(carry, items):
        q_seq, k_seq, v_seq, g_seq, rows, segment = items
        q_heads = q_seq.reshape(SEQ_LEN, H, HD)
        k_heads = jnp.repeat(k_seq.reshape(SEQ_LEN, KV, HD), per_group, axis=1)
        v_heads = jnp.repeat(v_seq.reshape(SEQ_LEN, KV, HD), per_group, axis=1)
        g_heads = g_seq.reshape(SEQ_LEN, H, HD)
        dq_all, dk_all, dv_all = attend(q_heads, k_heads, v_heads, g_heads, segment)
        rows_f = rows.astype(jnp.float32)
        q_term = jnp.einsum('lr,lhd->rhd', rows_f, dq_all.astype(jnp.float32)).reshape(RANK, H * HD)
        k_term = jnp.einsum('lr,lhd->rhd', rows_f, dk_all.astype(jnp.float32)).reshape(RANK, KV, per_group, HD).sum(axis=2)
        v_term = jnp.einsum('lr,lhd->rhd', rows_f, dv_all.astype(jnp.float32)).reshape(RANK, KV, per_group, HD).sum(axis=2)
        kv_term = jnp.stack([k_term, v_term], axis=1).reshape(RANK, 2 * KV * HD)
        return (carry[0] + q_term, carry[1] + kv_term), None

    start = (jnp.zeros((RANK, H * HD), jnp.float32), jnp.zeros((RANK, 2 * KV * HD), jnp.float32))
    (grad_q_proj, grad_kv_proj), unused = lax.scan(one_sequence, start, (queries, keys, values, grad_out, proj_in, segments))
    return grad_q_proj, grad_kv_proj
```

```python
import functools

import jax
import jax.numpy as jnp
from jax import lax
from jax.experimental import pallas as pl
from jax.experimental.pallas import tpu as pltpu
from jax.sharding import PartitionSpec as P

HD = 128
DOC = 128
NT = (((1,), (1,)), ((), ()))
NN = (((1,), (0,)), ((), ()))


def dot(a, b, dims):
    return lax.dot_general(a, b, dims, preferred_element_type=jnp.float32)


def bits_of(n):
    return n.bit_length() - 1


def stage_bits(dp, seq):
    assert dp == 1 << bits_of(dp) and seq == 1 << bits_of(seq)
    dp_bits = [("dp", b) for b in range(bits_of(dp))]
    seq_bits = [("seq", b) for b in range(bits_of(seq))]
    first, rest = dp_bits[:1], dp_bits[1:2] + seq_bits + dp_bits[2:]
    return [first] + [rest[i : i + 2] for i in range(0, len(rest), 2)]


def place_of(row, s, order):
    at = 0
    for axis, b in order:
        at = at * 2 + (((row >> (b - 1)) if axis == "dp" else (s >> b)) & 1)
    return at


def attention_kernel(blocks, per, kv_heads, dp, seq, order, *refs):
    seg_ref, q_ref, g_ref, k_ref, v_ref, pj_ref, hk_ref, hv_ref, hp_ref = refs[:9]
    keep_ref, send_ref, bias, pt, kt, dqt, dk, dv = refs[9:]
    B = hk_ref.shape[0]
    own = q_ref.shape[0]
    nb = own // B
    R = pj_ref.shape[1]
    f32, bf = jnp.float32, jnp.bfloat16
    scale = HD**-0.5
    to_exp2 = scale * 1.4426950408889634
    key = lax.broadcasted_iota(jnp.int32, (B, B), 0)
    qry = lax.broadcasted_iota(jnp.int32, (B, B), 1)
    cur = key <= qry
    cur2 = jnp.concatenate([cur, cur], axis=1)
    group = pl.program_id(0)
    r = R // dp

    @pl.when(group == 0)
    def _():
        dev = lax.axis_index("seq")
        low = lax.axis_index("dp") % 2
        for n in range(nb + 1):
            rows = (hp_ref[...] if n == 0 else pj_ref[(n - 1) * B : n * B]).astype(f32).T
            rows = rows.reshape(dp // 2, 2, r, B)
            for half in range(2):
                part = jnp.where(low == half, rows[:, 0], rows[:, 1]).reshape(R // 2, B)
                pt[half * (R // 2) : (half + 1) * (R // 2), n * B : (n + 1) * B] = part.astype(bf)
        for n in blocks:
            blk = dev * nb + n
            seg_cur = seg_ref[:, pl.ds(pl.multiple_of(blk * B, B), B)]
            prev = jnp.maximum(blk - 1, 0)
            seg_prev = seg_ref[:, pl.ds(pl.multiple_of(prev * B, B), B)]
            seg_prev = jnp.where(blk > 0, seg_prev, -1)
            cur_c = jnp.broadcast_to(seg_cur, (B, B)).astype(f32)
            prev_c = jnp.broadcast_to(seg_prev, (B, B)).astype(f32)
            key_seg = jnp.where(cur, cur_c.T, prev_c.T)
            bias[n] = jnp.where(key_seg == cur_c, 0.0, -1e30)

    dk[...] = jnp.zeros_like(dk)
    dv[...] = jnp.zeros_like(dv)
    for n in range(nb + 1):
        kt[n] = (hk_ref[...] if n == 0 else k_ref[(n - 1) * B : n * B]).T

    def window(ref, halo, n):
        if n:
            return ref[(n - 1) * B : (n + 1) * B]
        return jnp.concatenate([halo[...], ref[:B]], axis=0)

    def cols(hp):
        return [slice((2 * hp + j) * HD, (2 * hp + j + 1) * HD) for j in range(2)]

    def stack(ref, n, hp):
        return jnp.concatenate([ref[n * B : (n + 1) * B, c] for c in cols(hp)], axis=0)

    def scores(n, hp):
        s2 = dot(window(k_ref, hk_ref, n), stack(q_ref, n, hp), NT)
        d2 = dot(window(v_ref, hv_ref, n), stack(g_ref, n, hp), NT)
        return s2, d2

    def soft(n, hp, s2, d2):
        b2 = jnp.concatenate([bias[n], bias[n]], axis=1)
        s = jnp.where(cur2, s2[B:], s2[:B]) + b2
        d = jnp.where(cur2, d2[B:], d2[:B])
        m = jnp.max(s, axis=0, keepdims=True)
        p = jnp.exp2((s - m) * to_exp2)
        total = jnp.sum(p, axis=0, keepdims=True)
        p = p * (1.0 / total)
        delta = jnp.sum(p * d, axis=0, keepdims=True)
        ds = (p * (d - delta)).astype(bf)
        pb = p.astype(bf)
        z = jnp.zeros_like(pb)
        p2 = jnp.concatenate([jnp.where(cur2, z, pb), jnp.where(cur2, pb, z)], axis=0)
        ds2 = jnp.concatenate([jnp.where(cur2, z, ds), jnp.where(cur2, ds, z)], axis=0)
        return p2, ds2

    def gradients(n, hp, p2, ds2):
        rows = slice(n * B, (n + 2) * B)
        dk[rows] += dot(ds2, stack(q_ref, n, hp), NN)
        dv[rows] += dot(p2, stack(g_ref, n, hp), NN)
        kt2 = jnp.concatenate([kt[n], kt[n + 1]], axis=1)
        dq = dot(kt2, ds2, NN).astype(bf)
        for j, c in enumerate(cols(hp)):
            dqt[c, n * B : (n + 1) * B] = dq[:, j * B : (j + 1) * B]

    steps = [(n, hp) for hp in range(per // 2) for n in blocks]
    ready = scores(*steps[0])
    done = None
    for i, step in enumerate(steps):
        after = scores(*steps[i + 1]) if i + 1 < len(steps) else None
        if done is not None:
            gradients(*done)
        done = step + soft(*step, *ready)
        ready = after
    gradients(*done)

    def store(value, s, lane, width):
        for row in range(dp // 2):
            at = place_of(row, s, order)
            keep_ref[at, :, lane : lane + width] = value[row * r : (row + 1) * r]
            send_ref[at, :, lane : lane + width] = value[R // 2 + row * r : R // 2 + (row + 1) * r]

    lo, hi = blocks[0] * B, (blocks[-1] + 1) * B
    q_width = per * kv_heads * HD // seq
    kv_width = 2 * kv_heads * HD // seq
    tok = pt[:, lo + B : hi + B]
    wide = min(2 * HD, q_width)
    for j in range(0, per * HD, wide):
        value = (dot(tok, dqt[j : j + wide, lo:hi], NT) * scale).astype(bf)
        store(value, group * (per * HD // q_width) + j // q_width, j % q_width, wide)
    tok = pt[:, lo : hi + B]
    for which, ref in enumerate((dk, dv)):
        value = dot(tok, ref[lo : hi + B].astype(bf), NN)
        value = (value * scale if which == 0 else value).astype(bf)
        for j in range(0, HD, kv_width):
            s = which * (seq // 2) + group * (HD // kv_width) + j // kv_width
            store(value[:, j : j + kv_width], s, q_width, kv_width)


def attention(blocks, kv_heads, dp, seq, order, queries, grad_out, keys, values, proj, halo, segments):
    hk, hv, hp = halo
    B = hk.shape[0]
    own, width = queries.shape
    per = width // HD // kv_heads
    nb = own // B
    R = proj.shape[1]
    pieces = dp // 2 * seq
    piece = (pieces, R // dp, width // seq + 2 * kv_heads * HD // seq)
    bf, f32 = jnp.bfloat16, jnp.float32
    whole = lambda i: (0, 0)
    col = lambda i: (0, i)
    call = pl.pallas_call(
        functools.partial(attention_kernel, blocks, per, kv_heads, dp, seq, order),
        grid=(kv_heads,),
        in_specs=[
            pl.BlockSpec(segments.shape, whole),
            pl.BlockSpec((own, per * HD), col),
            pl.BlockSpec((own, per * HD), col),
            pl.BlockSpec((own, HD), col),
            pl.BlockSpec((own, HD), col),
            pl.BlockSpec((own, R), whole),
            pl.BlockSpec((B, HD), col),
            pl.BlockSpec((B, HD), col),
            pl.BlockSpec((B, R), whole),
        ],
        out_specs=[pl.BlockSpec(piece, lambda i: (0, 0, 0))] * 2,
        out_shape=[jax.ShapeDtypeStruct(piece, bf)] * 2,
        scratch_shapes=[
            pltpu.VMEM((nb, B, B), f32),
            pltpu.VMEM((R, own + B), bf),
            pltpu.VMEM((nb + 1, HD, B), bf),
            pltpu.VMEM((per * HD, own), bf),
            pltpu.VMEM((own + B, HD), f32),
            pltpu.VMEM((own + B, HD), f32),
        ],
        name="attention",
    )
    return call(segments, queries, grad_out, keys, values, proj, hk, hv, hp)


def exchange(value, dp, seq, flips):
    dp_flip = sum(1 << b for axis, b in flips if axis == "dp")
    seq_flip = sum(1 << b for axis, b in flips if axis == "seq")
    pairs = [
        (d * seq + s, (d ^ dp_flip) * seq + (s ^ seq_flip)) for d in range(dp) for s in range(seq)
    ]
    return lax.ppermute(value, ("dp", "seq"), pairs)


def scatter_sum(value, dp, seq, bits):
    f32, bf = jnp.float32, jnp.bfloat16
    parts = value.reshape((1 << len(bits), -1) + value.shape[1:])
    mine = 0
    for axis, b in bits:
        mine = mine * 2 + ((lax.axis_index(axis) >> b) & 1)
    total = lax.dynamic_index_in_dim(parts, mine, 0, keepdims=False).astype(f32)
    for flip in range((1 << len(bits)) - 1, 0, -1):
        flips = [bit for i, bit in enumerate(bits) if (flip >> (len(bits) - 1 - i)) & 1]
        sent = lax.dynamic_index_in_dim(parts, mine ^ flip, 0, keepdims=False).astype(bf)
        total = total + exchange(sent, dp, seq, flips).astype(f32)
    return total


def on_device(dp, seq, queries, keys, values, grad_out, proj_in, segments):
    own = queries.shape[1]
    kv_heads = keys.shape[2] // HD
    B = DOC
    nb = own // B
    bf = jnp.bfloat16
    tail = jnp.concatenate([keys[0, own - B :], values[0, own - B :], proj_in[0, own - B :]], axis=1)
    tail = lax.ppermute(tail, "seq", [(i, i + 1) for i in range(seq - 1)])
    kw = keys.shape[2]
    halo = (tail[:, :kw], tail[:, kw : 2 * kw], tail[:, 2 * kw :])
    stages = stage_bits(dp, seq)
    order = [bit for bits in stages[1:] for bit in bits]
    keep, send = attention(
        tuple(range(nb)), kv_heads, dp, seq, order,
        queries[0], grad_out[0], keys[0], values[0], proj_in[0], halo, segments,
    )
    total = keep.astype(jnp.float32) + exchange(send, dp, seq, stages[0]).astype(jnp.float32)
    for bits in stages[1:]:
        total = scatter_sum(total, dp, seq, bits)
    total = total[0]
    q_width = queries.shape[2] // seq
    return total[:, :q_width], total[:, q_width:]


def solution(mesh):
    dp, seq = mesh.shape["dp"], mesh.shape["seq"]
    split = P("dp", "seq", None)
    return jax.shard_map(
        functools.partial(on_device, dp, seq),
        mesh=mesh,
        in_specs=(split,) * 5 + (P("dp", None),),
        out_specs=(P("dp", "seq"), P("dp", "seq")),
        check_vma=False,
    )
```

```python
import functools

import jax
import jax.numpy as jnp
from jax import lax
from jax.experimental import pallas as pl
from jax.experimental.pallas import tpu as pltpu
from jax.sharding import PartitionSpec as P

HD = 128
DOC = 128
NT = (((1,), (1,)), ((), ()))
NN = (((1,), (0,)), ((), ()))


def dot(a, b, dims):
    return lax.dot_general(a, b, dims, preferred_element_type=jnp.float32)


def bits_of(n):
    return n.bit_length() - 1


def stage_bits(dp, seq):
    assert dp == 1 << bits_of(dp) and seq == 1 << bits_of(seq)
    dp_bits = [("dp", b) for b in range(bits_of(dp))]
    seq_bits = [("seq", b) for b in range(bits_of(seq))]
    first, rest = dp_bits[:1], dp_bits[1:2] + seq_bits + dp_bits[2:]
    return [first] + [rest[i : i + 2] for i in range(0, len(rest), 2)]


def place_of(row, s, order):
    at = 0
    for axis, b in order:
        at = at * 2 + (((row >> (b - 1)) if axis == "dp" else (s >> b)) & 1)
    return at


def pack_kernel(k_ref, v_ref, pj_ref, out_ref):
    kw = k_ref.shape[1]
    out_ref[:, :kw] = k_ref[...]
    out_ref[:, kw : 2 * kw] = v_ref[...]
    out_ref[:, 2 * kw :] = pj_ref[...]


def pack(keys, values, proj, B):
    last = lambda i: (keys.shape[0] // B - 1, 0)
    width = 2 * keys.shape[1] + proj.shape[1]
    return pl.pallas_call(
        pack_kernel,
        grid=(1,),
        in_specs=[pl.BlockSpec((B, a.shape[1]), last) for a in (keys, values, proj)],
        out_specs=pl.BlockSpec((B, width), lambda i: (0, 0)),
        out_shape=jax.ShapeDtypeStruct((B, width), keys.dtype),
        name="pack",
    )(keys, values, proj)


def attention_kernel(plan, *refs):
    steps, first, sizes, order = plan
    kv_heads, dp, seq = sizes
    seg_ref, q_ref, g_ref, k_ref, v_ref, pj_ref = refs[:6]
    refs = refs[6:]
    hk_ref = hv_ref = hp_ref = qa_ref = kva_ref = None
    if not first:
        hk_ref, hv_ref, hp_ref = refs[:3]
        refs = refs[3:]
        if len(refs) == 10:
            qa_ref, kva_ref = refs[:2]
            refs = refs[2:]
    out_a, out_b, bias, pt, kt, dqt, dk, dv = refs
    B = DOC
    own, width = q_ref.shape
    nb = own // B
    R = pj_ref.shape[1]
    f32, bf = jnp.float32, jnp.bfloat16
    scale = HD**-0.5
    to_exp2 = scale * 1.4426950408889634
    key = lax.broadcasted_iota(jnp.int32, (B, B), 0)
    qry = lax.broadcasted_iota(jnp.int32, (B, B), 1)
    cur = key <= qry
    cur2 = jnp.concatenate([cur, cur], axis=1)
    group = pl.program_id(0)
    r = R // dp
    blocks = sorted({n for n, _ in steps})
    key_blocks = range(blocks[0], nb + 1)

    def block_of(ref, halo, n):
        return ref[(n - 1) * B : n * B] if n else halo[...]

    @pl.when(group == 0)
    def _():
        dev = lax.axis_index("seq")
        low = lax.axis_index("dp") % 2
        for n in key_blocks:
            rows = block_of(pj_ref, hp_ref, n).astype(f32).T
            rows = rows.reshape(dp // 2, 2, r, B)
            for half in range(2):
                part = jnp.where(low == half, rows[:, 0], rows[:, 1]).reshape(R // 2, B)
                pt[half * (R // 2) : (half + 1) * (R // 2), n * B : (n + 1) * B] = part.astype(bf)
        for n in blocks:
            blk = dev * nb + n
            seg_cur = seg_ref[:, pl.ds(pl.multiple_of(blk * B, B), B)]
            prev = jnp.maximum(blk - 1, 0)
            seg_prev = seg_ref[:, pl.ds(pl.multiple_of(prev * B, B), B)]
            seg_prev = jnp.where(blk > 0, seg_prev, -1)
            cur_c = jnp.broadcast_to(seg_cur, (B, B)).astype(f32)
            prev_c = jnp.broadcast_to(seg_prev, (B, B)).astype(f32)
            key_seg = jnp.where(cur, cur_c.T, prev_c.T)
            bias[n] = jnp.where(key_seg == cur_c, 0.0, -1e30)

    dk[...] = jnp.zeros_like(dk)
    dv[...] = jnp.zeros_like(dv)
    for n in key_blocks:
        kt[n] = block_of(k_ref, hk_ref, n).T

    def window(ref, halo, n):
        if n:
            return ref[(n - 1) * B : (n + 1) * B]
        return jnp.concatenate([halo[...], ref[:B]], axis=0)

    def cols(hp):
        return [slice((2 * hp + j) * HD, (2 * hp + j + 1) * HD) for j in range(2)]

    def stack(ref, n, hp):
        return jnp.concatenate([ref[n * B : (n + 1) * B, c] for c in cols(hp)], axis=0)

    def scores(n, hp):
        s2 = dot(window(k_ref, hk_ref, n), stack(q_ref, n, hp), NT)
        d2 = dot(window(v_ref, hv_ref, n), stack(g_ref, n, hp), NT)
        return s2, d2

    def soft(n, hp, s2, d2):
        b2 = jnp.concatenate([bias[n], bias[n]], axis=1)
        s = jnp.where(cur2, s2[B:], s2[:B]) + b2
        d = jnp.where(cur2, d2[B:], d2[:B])
        m = jnp.max(s, axis=0, keepdims=True)
        p = jnp.exp2((s - m) * to_exp2)
        total = jnp.sum(p, axis=0, keepdims=True)
        p = p * (1.0 / total)
        delta = jnp.sum(p * d, axis=0, keepdims=True)
        ds = (p * (d - delta)).astype(bf)
        pb = p.astype(bf)
        z = jnp.zeros_like(pb)
        p2 = jnp.concatenate([jnp.where(cur2, z, pb), jnp.where(cur2, pb, z)], axis=0)
        ds2 = jnp.concatenate([jnp.where(cur2, z, ds), jnp.where(cur2, ds, z)], axis=0)
        return p2, ds2

    def gradients(n, hp, p2, ds2):
        rows = slice(n * B, (n + 2) * B)
        dk[rows] += dot(ds2, stack(q_ref, n, hp), NN)
        dv[rows] += dot(p2, stack(g_ref, n, hp), NN)
        kt2 = jnp.concatenate([kt[n], kt[n + 1]], axis=1)
        dq = dot(kt2, ds2, NN).astype(bf)
        for j, c in enumerate(cols(hp)):
            dqt[c, n * B : (n + 1) * B] = dq[:, j * B : (j + 1) * B]

    ready = scores(*steps[0])
    done = None
    for i, step in enumerate(steps):
        after = scores(*steps[i + 1]) if i + 1 < len(steps) else None
        if done is not None:
            gradients(*done)
        done = step + soft(*step, *ready)
        ready = after
    gradients(*done)

    def store(value, s, lane, size):
        for row in range(dp // 2):
            at = place_of(row, s, order)
            out_a[at, :, lane : lane + size] = value[row * r : (row + 1) * r].astype(bf)
            out_b[at, :, lane : lane + size] = value[R // 2 + row * r : R // 2 + (row + 1) * r].astype(bf)

    per = width // HD
    q_width = per * kv_heads * HD // seq
    kv_width = 2 * kv_heads * HD // seq
    wide = min(2 * HD, q_width)
    for j in range(0, width, wide):
        mine = sorted(n for n, hp in steps if hp == j // (2 * HD))
        lo, hi = mine[0] * B, (mine[-1] + 1) * B
        value = dot(pt[:, lo + B : hi + B], dqt[j : j + wide, lo:hi], NT) * scale
        if first:
            out_a[:, j : j + wide] = value.astype(out_a.dtype)
            continue
        if qa_ref is not None and j < qa_ref.shape[1]:
            value = value + qa_ref[:, j : j + wide].astype(f32)
        store(value, group * (width // q_width) + j // q_width, j % q_width, wide)
    tok = pt[:, blocks[0] * B :]
    for which, ref in enumerate((dk, dv)):
        value = dot(tok, ref[blocks[0] * B :].astype(bf), NN)
        value = value * scale if which == 0 else value
        if first:
            out_b[:, which * HD : (which + 1) * HD] = value
            continue
        if kva_ref is not None:
            value = value + kva_ref[:, which * HD : (which + 1) * HD]
        for j in range(0, HD, kv_width):
            s = which * (seq // 2) + group * (HD // kv_width) + j // kv_width
            store(value[:, j : j + kv_width], s, q_width, kv_width)


def attention(steps, sizes, order, queries, grad_out, keys, values, proj, segments, halo=None, before=()):
    kv_heads, dp, seq = sizes
    first = halo is None
    B = DOC
    own, width = queries.shape
    cut = width // kv_heads // (2 if first else 1)
    nb = own // B
    R, kw = proj.shape[1], keys.shape[1]
    bf, f32 = jnp.bfloat16, jnp.float32
    whole = lambda i: (0, 0)
    col = lambda i: (0, i)
    heads = (lambda i: (0, 2 * i)) if first else col
    in_specs = [
        pl.BlockSpec(segments.shape, whole),
        pl.BlockSpec((own, cut), heads),
        pl.BlockSpec((own, cut), heads),
        pl.BlockSpec((own, HD), col),
        pl.BlockSpec((own, HD), col),
        pl.BlockSpec((own, R), whole),
    ]
    args = [segments, queries, grad_out, keys, values, proj]
    if first:
        out_specs = [pl.BlockSpec((R, cut), col), pl.BlockSpec((R, 2 * HD), col)]
        out_shape = [
            jax.ShapeDtypeStruct((R, cut * kv_heads), bf),
            jax.ShapeDtypeStruct((R, 2 * HD * kv_heads), f32),
        ]
    else:
        in_specs += [
            pl.BlockSpec((B, HD), col),
            pl.BlockSpec((B, HD), lambda i: (0, kv_heads + i)),
            pl.BlockSpec((B, R), lambda i: (0, 2 * kw // R)),
        ]
        args += [halo] * 3
        piece = (dp // 2 * seq, R // dp, width // seq + 2 * kw // seq)
        out_specs = [pl.BlockSpec(piece, lambda i: (0, 0, 0))] * 2
        out_shape = [jax.ShapeDtypeStruct(piece, bf)] * 2
        for a in before:
            in_specs.append(pl.BlockSpec((R, a.shape[1] // kv_heads), col))
            args.append(a)
    call = pl.pallas_call(
        functools.partial(attention_kernel, (steps, first, sizes, order)),
        grid=(kv_heads,),
        in_specs=in_specs,
        out_specs=out_specs,
        out_shape=out_shape,
        scratch_shapes=[
            pltpu.VMEM((nb, B, B), f32),
            pltpu.VMEM((R, own + B), bf),
            pltpu.VMEM((nb + 1, HD, B), bf),
            pltpu.VMEM((cut, own), bf),
            pltpu.VMEM((own + B, HD), f32),
            pltpu.VMEM((own + B, HD), f32),
        ],
        cost_estimate=pl.CostEstimate(
            flops=len(steps) * kv_heads * 100_000_000, bytes_accessed=own * cut * kv_heads * 4, transcendentals=0
        ),
        name="inner" if first else "attention",
    )
    return call(*args)


def exchange(value, dp, seq, flips):
    dp_flip = sum(1 << b for axis, b in flips if axis == "dp")
    seq_flip = sum(1 << b for axis, b in flips if axis == "seq")
    pairs = [
        (d * seq + s, (d ^ dp_flip) * seq + (s ^ seq_flip)) for d in range(dp) for s in range(seq)
    ]
    return lax.ppermute(value, ("dp", "seq"), pairs)


def add_up(values):
    total = values[0].astype(jnp.float32)
    for value in values[1:]:
        total = total + value.astype(jnp.float32)
    return total


def scatter_sum(values, dp, seq, bits):
    mine = 0
    for axis, b in bits:
        mine = mine * 2 + ((lax.axis_index(axis) >> b) & 1)

    def part(i):
        parts = [v.reshape((1 << len(bits), -1) + v.shape[1:]) for v in values]
        return add_up([lax.dynamic_index_in_dim(v, i, 0, keepdims=False) for v in parts])

    terms = []
    for flip in range((1 << len(bits)) - 1, 0, -1):
        flips = [bit for i, bit in enumerate(bits) if (flip >> (len(bits) - 1 - i)) & 1]
        terms.append(exchange(part(mine ^ flip).astype(jnp.bfloat16), dp, seq, flips))
    return [part(mine)] + terms


def on_device(dp, seq, queries, keys, values, grad_out, proj_in, segments):
    own = queries.shape[1]
    kv_heads = keys.shape[2] // HD
    B = DOC
    nb = own // B
    pairs = queries.shape[2] // HD // kv_heads // 2
    q, g, k, v, pj = (a[0] for a in (queries, grad_out, keys, values, proj_in))
    halo = lax.ppermute(pack(k, v, pj, B), "seq", [(i, i + 1) for i in range(seq - 1)])
    stages = stage_bits(dp, seq)
    order = [bit for bits in stages[1:] for bit in bits]
    sizes = (kv_heads, dp, seq)
    early = [(n, hp) for hp in range(pairs // 2) for n in range(1, nb)]
    late = [(n, hp) for hp in range(pairs) for n in range(nb) if (n, hp) not in early]
    before = attention(early, sizes, order, q, g, k, v, pj, segments) if early else ()
    keep, send = attention(late, sizes, order, q, g, k, v, pj, segments, halo, before)
    terms = [keep, exchange(send, dp, seq, stages[0])]
    for bits in stages[1:]:
        terms = scatter_sum(terms, dp, seq, bits)
    q_width = queries.shape[2] // seq
    return add_up([t[0, :, :q_width] for t in terms]), add_up([t[0, :, q_width:] for t in terms])


def solution(mesh):
    dp, seq = mesh.shape["dp"], mesh.shape["seq"]
    split = P("dp", "seq", None)
    return jax.shard_map(
        functools.partial(on_device, dp, seq),
        mesh=mesh,
        in_specs=(split,) * 5 + (P("dp", None),),
        out_specs=(P("dp", "seq"), P("dp", "seq")),
        check_vma=False,
    )
```
